256 devices in a mesh: walker: 64 (over x_hi, y, z), freq: 4 (over x_lo, core).
Axes of the slice: x: 4 (x_hi: 2, x_lo: 2; x = x_hi * 2 + x_lo), y: 4, z: 8, core: 2. Of those that a mesh axis runs over, the one named last changes fastest.
Arguments:
- green_up_blocks: bfloat16 [64, 1, 4, 4288], P('walker', None, 'freq'), may hold values from -6 to 6
- green_down_blocks: bfloat16 [64, 1, 4, 4288], P('walker', None, 'freq'), may hold values from -6 to 6
- nu_index: int32 [4], P('freq'), may hold values from 0 to 3, each once
- q_index: int32 [4], P('freq'), may hold values from 0 to 63
- source: float32 [4, 4096], P('freq', 'walker'), may hold values from -6 to 6
Outputs:
- g4: float32 [4, 4096, 4096], P('freq', 'walker')
- response: float32 [4, 4096], P('freq', 'walker')
The draws below stay inside these ranges and needn't reach their ends.
All inputs are finite; a program needn't handle non-finite values.
Results may differ from the reference program's by a relative error of at most 0.004.
Values may be sent and summed in bfloat16 or wider, within the bound.
No kernel may reach another device: no remote copies, remote signals or barrier semaphores. Data moves between devices by JAX's collectives and lax.ppermute only.
A program may use at most 64 MiB of HBM per device.

```python
import math
import jax
import jax.numpy as jnp
from jax import lax

SIDE = 8
CLUSTER_MOMENTUM = 64
ORBITAL_COUNT = 4
W = 64
NU = 4
WALKER_SAMPLES = 1
ITERS = 2
WALKER_COUNT = 64
BLOCK_FREQUENCY = 67


def set_ends(values, own_key, least, high):
    dims = values.shape
    place = [jax.random.randint(jax.random.fold_in(own_key, axis), (), 0, dims[axis]) for axis in range(len(dims))]
    values = values.at[tuple(place)].set(least)
    longest = dims.index(max(dims))
    place[longest] = (place[longest] + 1) % dims[longest]
    return values.at[tuple(place)].set(high)


def block_scale(stream_key, dims, split, smallest, largest):
    gain = 1.0
    for dim, shards_of in split:
        draws = jax.random.uniform(jax.random.fold_in(jax.random.fold_in(stream_key, 6), dim), (shards_of,), jnp.float32, smallest / len(split), largest / len(split))
        gain = gain * jnp.repeat(jnp.exp(draws), dims[dim] // shards_of).reshape((-1,) + (1,) * (len(dims) - 1 - dim))
    return gain


def centred(rng, dims, spread, limit, shards=(), kind=jnp.bfloat16):
    entries = spread * jax.random.normal(rng, dims, jnp.float32)
    if shards:
        entries = entries * block_scale(rng, dims, shards, -0.22, 0.18)
    return jnp.clip(entries, -limit, limit).astype(kind)


def setup_inputs(seed: int = 0) -> dict:
    splits = jax.random.split(jax.random.key(seed), 6)
    green_up_blocks = centred(splits[0], (WALKER_COUNT, WALKER_SAMPLES, ORBITAL_COUNT, CLUSTER_MOMENTUM * BLOCK_FREQUENCY), 1.0, 6.0, ((0, 64), (2, 4)))
    green_down_blocks = centred(splits[1], (WALKER_COUNT, WALKER_SAMPLES, ORBITAL_COUNT, CLUSTER_MOMENTUM * BLOCK_FREQUENCY), 1.0, 6.0, ((0, 64), (2, 4)))
    nu_index = jax.random.permutation(splits[2], NU).astype(jnp.int32)
    q_index = set_ends(jax.random.randint(splits[3], (NU,), 0, CLUSTER_MOMENTUM), jax.random.fold_in(splits[3], 1), 0, CLUSTER_MOMENTUM - 1).astype(jnp.int32)
    source = centred(splits[4], (NU, CLUSTER_MOMENTUM * W), 1.0, 6.0, ((0, 4), (1, 64)), jnp.float32)
    return {"green_up_blocks": green_up_blocks, "green_down_blocks": green_down_blocks, "nu_index": nu_index, "q_index": q_index, "source": source}


def cluster_sum(sites, shift):
    return (sites // SIDE + shift // SIDE) % SIDE * SIDE + (sites % SIDE + shift % SIDE) % SIDE

def products(block, sites, shift, offset):
    moved = cluster_sum(sites, shift)
    base = jnp.take(block, sites, axis=1)[:, :, :W].astype(jnp.float32)
    other = lax.dynamic_slice_in_dim(jnp.take(block, moved, axis=1), offset, W, 2).astype(jnp.float32)
    return (base * other).astype(jnp.bfloat16).reshape(block.shape[0], sites.shape[0] * W)

def reference(green_up_blocks, green_down_blocks, nu_index, q_index, source):
    sample_count = WALKER_COUNT * WALKER_SAMPLES * ORBITAL_COUNT
    norm = 1.0 / math.sqrt(sample_count)
    scale = 1.0 / (2.0 * math.sqrt(CLUSTER_MOMENTUM * W))
    ups = green_up_blocks.reshape(sample_count, CLUSTER_MOMENTUM, W + NU - 1)
    downs = green_down_blocks.reshape(sample_count, CLUSTER_MOMENTUM, W + NU - 1)
    every = jnp.arange(CLUSTER_MOMENTUM, dtype=jnp.int32)

    def one(packed):
        offset, shift, start = packed
        left = products(ups, every, shift, offset).astype(jnp.float32)
        right = products(downs, every, shift, offset).astype(jnp.float32)
        kernel = jnp.dot(left.T, right, precision=lax.Precision.HIGHEST) * norm
        current = start
        for step in range(ITERS):
            current = start + scale * jnp.dot(current, kernel, precision=lax.Precision.HIGHEST)
        return (kernel, current)
    kernels, answers = lax.map(one, (nu_index, q_index, source))
    return (kernels, answers)
```

```python
import math

import jax
import jax.numpy as jnp
from jax import lax
from jax.experimental import pallas as pl
from jax.experimental.pallas import tpu as pltpu
from jax.sharding import Mesh, PartitionSpec as P

SIDE = 8
CLUSTER_MOMENTUM = 64
W = 64
NU = 4
ITERS = 2
EXTENT = W + NU - 1
SITES = CLUSTER_MOMENTUM * W
RUN = SIDE * EXTENT
GROUP = 640
SPIN = SIDE * GROUP
OUT = SIDE * W
CHIPS = ("xh", "y", "z", "xl")
LANES = 128
PLANE = GROUP // LANES


def selector(turn, offset):
    row = lax.broadcasted_iota(jnp.int32, (GROUP, OUT), 0)
    col = lax.broadcasted_iota(jnp.int32, (GROUP, OUT), 1)
    want = ((col // W + turn) & (SIDE - 1)) * EXTENT + (col & (W - 1)) + offset
    return jnp.where(row == want, 1.0, 0.0).astype(jnp.bfloat16)


def kernel(where_ref, mine_ref, theirs_ref, s_ref, own_ref, g4_ref, out_ref, up_ref, down_ref, t_ref):
    jump, turn, offset, site = where_ref[0], where_ref[1], where_ref[2], where_ref[3]
    half = mine_ref.shape[0]
    rows = 2 * half
    here = selector(0, 0)
    there = selector(turn, offset)
    f32 = jnp.float32

    def load(group, spin):
        cols = pl.ds(pl.multiple_of(group * GROUP + spin * SPIN, LANES), GROUP)
        return [mine_ref[:, cols], theirs_ref[:, cols]]

    def step(a, carry):
        moved = (a + jump) & (SIDE - 1)
        lhs = jnp.concatenate(load(a, 0) + load(a, 1), axis=0)
        rhs = jnp.concatenate(load(moved, 0) + load(moved, 1), axis=0)
        base = jnp.dot(lhs, here, preferred_element_type=f32)
        other = jnp.dot(rhs, there, preferred_element_type=f32)
        prod = (base * other).astype(jnp.bfloat16)
        cols = pl.ds(pl.multiple_of(a * OUT, LANES), OUT)
        up_ref[:, cols] = prod[:rows]
        down_ref[:, cols] = prod[rows:]
        return carry

    lax.fori_loop(0, SIDE, step, 0)
    norm = 1.0 / math.sqrt(rows)
    scale = norm / (2.0 * math.sqrt(SITES))
    pair = pl.ds(pl.multiple_of((site // 2) * LANES, LANES), LANES)
    odd = site & 1
    t_ref[...] = up_ref[:, pair].astype(f32).T
    left = t_ref[pl.ds(pl.multiple_of(odd * W, W), W), :].astype(jnp.bfloat16)
    nt = (((1,), (1,)), ((), ()))
    g4_ref[0] = jnp.dot(left, down_ref[...], preferred_element_type=f32) * norm
    s = s_ref[...]
    hi = s.astype(jnp.bfloat16)
    rest = s - hi.astype(f32)
    mid = rest.astype(jnp.bfloat16)
    lo = (rest - mid.astype(f32)).astype(jnp.bfloat16)
    up = up_ref[...]
    t0 = sum(lax.dot_general(p, up, nt, preferred_element_type=f32) for p in (hi, mid, lo))
    gram = lax.dot_general(down_ref[...], up, nt, preferred_element_type=f32)
    t0_col = t0.T[:, :1]
    t_row = t0[:1]
    for _ in range(ITERS - 1):
        t_row = t0[:1] + scale * jnp.sum(gram * t0_col, axis=0, keepdims=True)
    t_col = jnp.broadcast_to(t_row, t0.shape).T[:, :1]
    add = jnp.sum(down_ref[:, pair].astype(f32) * t_col, axis=0, keepdims=True)
    add = jnp.where(odd == 1, add[:, W:], add[:, :W])
    out_ref[...] = own_ref[...] + scale * add


def pieces(values):
    first = lax.reduce_precision(values, 8, 7)
    rest = values - first
    second = lax.reduce_precision(rest, 8, 7)
    third = lax.reduce_precision(rest - second, 8, 7)
    return [p.astype(jnp.bfloat16) for p in (first, second, third)]


def spread(block, extra):
    room = GROUP - RUN
    tail = jnp.zeros((SIDE, room), jnp.bfloat16)
    if extra is not None:
        tail = jnp.pad(jnp.concatenate(extra, 0), ((0, SIDE - len(extra)), (0, room - W)))
    return jnp.concatenate([block.reshape(SIDE, RUN), tail], 1).reshape(SPIN // LANES, LANES)


def shards(green_up_blocks, green_down_blocks, nu_index, q_index, source):
    parts = pieces(source)
    block = jnp.concatenate([spread(green_up_blocks, parts), spread(green_down_blocks, None)], 0)
    chips = lax.axis_size(CHIPS)
    depth = block.shape[0]
    mine = lax.all_to_all(
        jnp.broadcast_to(block[None], (chips,) + block.shape), CHIPS, 0, 0, tiled=True
    )
    planes = mine.reshape(chips // 2, 2, depth, LANES)
    planes = lax.dynamic_index_in_dim(planes, lax.axis_index("xl"), 1, False)
    at = RUN - (PLANE - 1) * LANES
    s = sum(
        planes[:, (g + 1) * PLANE - 1, at : at + W].astype(jnp.float32) for g in (2, 1, 0)
    ).reshape(1, SITES)
    mine = mine.reshape(chips, depth * LANES)
    theirs = lax.ppermute(mine, "c", [(0, 1), (1, 0)])
    site = lax.axis_index(("xh", "y", "z"))
    where = jnp.stack([q_index[0] // SIDE, q_index[0] % SIDE, nu_index[0], site])
    vmem = pl.BlockSpec(memory_space=pltpu.VMEM)
    return pl.pallas_call(
        kernel,
        in_specs=[pl.BlockSpec(memory_space=pltpu.SMEM)] + [vmem] * 4,
        out_specs=[vmem, vmem],
        out_shape=[
            jax.ShapeDtypeStruct((1, W, SITES), jnp.float32),
            jax.ShapeDtypeStruct((1, W), jnp.float32),
        ],
        scratch_shapes=[
            pltpu.VMEM((2 * chips, SITES), jnp.bfloat16),
            pltpu.VMEM((2 * chips, SITES), jnp.bfloat16),
            pltpu.VMEM((LANES, 2 * chips), jnp.float32),
        ],
    )(where.astype(jnp.int32), mine, theirs, jnp.broadcast_to(s, (8, SITES)), source)


def solution(mesh):
    fine = Mesh(mesh.devices.reshape(2, 4, 8, 2, 2), ("xh", "y", "z", "xl", "c"))
    walker, freq = ("xh", "y", "z"), ("xl", "c")
    in_specs = (
        P(walker, None, freq, None),
        P(walker, None, freq, None),
        P(freq),
        P(freq),
        P(freq, walker),
    )
    out_specs = (P(freq, walker, None), P(freq, walker))
    return jax.shard_map(shards, mesh=fine, in_specs=in_specs, out_specs=out_specs, check_vma=False)
```
